128 devices in a mesh: dp: 8 (over z, x_hi), ind: 16 (over y, x_lo, core).
Axes of the slice: x: 4 (x_hi: 2, x_lo: 2; x = x_hi * 2 + x_lo), y: 4, z: 4, core: 2. Of those that a mesh axis runs over, the one named last changes fastest.
Arguments:
- factor_rows: bfloat16 [8192, 8192], P('ind'), may hold values from -0.0625 to 0.0625
- diag_inverse: float32 [8192, 512], P('ind'), may hold values from -0.2 to 1.5, as said below
- inducing: float32 [8, 8192], P(None, 'ind'), may hold values from -6 to 6
- data_points: float32 [8, 2048], P(None, 'dp'), may hold values from -6 to 6
- lengthscale: float32 [8], replicated, may hold values from 1.5 to 4
- carried: float32 [8192, 2048], P('ind', 'dp'), may hold values from -4 to 4
- block_order: int32 [16], replicated, may hold values from 0 to 15, each once
- panel_pair: int32 [2], replicated, may hold values from 0 to 15, as said below
Outputs:
- solved: bfloat16 [8192, 2048], P('ind', 'dp')
- gram: float32 [1024, 1024], P('dp')
The draws below stay inside these ranges and needn't reach their ends.
Inputs may be any that keep to these rules, and one draw needn't show every extreme that they name: `diag_inverse`: each 512 x 512 block is lower triangular with its diagonal between 0.5 and 1.5. `panel_pair`: the two positions differ, and one of them is the last position 15.
All inputs are finite; a program needn't handle non-finite values.
Results may differ from the reference program's by a relative error of at most 0.0095.
Values may be sent and summed in bfloat16 or wider, within the bound.
A program may use at most 64 MiB of HBM per device.

```python
import math
import jax
import jax.numpy as jnp
from jax import lax

BLOCK = 512
DIM = 8
WB = 16
WROWS = 8192
NTOT = 2048


def draw_diag_inverse(key, part):
    key_diag, key_off = jax.random.split(jax.random.fold_in(key, 11))
    diagonal = jnp.exp(jax.random.uniform(key_diag, (WB, BLOCK), jnp.float32, jnp.log(0.5), jnp.log(1.5)))
    offdiag = jax.random.normal(key_off, (WB, BLOCK, BLOCK), jnp.float32) * (0.5 / jnp.sqrt(1.0 * BLOCK))
    offdiag = jnp.clip(offdiag, -0.19, 0.19)
    lower = jnp.tril(offdiag, -1)
    eye_block = jnp.eye(BLOCK, dtype=jnp.float32)
    mats = lower + diagonal[:, :, None] * eye_block[None, :, :]
    return mats.reshape(WB * BLOCK, BLOCK)


def draw_panel_pair(key, part):
    key_other, key_coin = jax.random.split(jax.random.fold_in(key, 23))
    other_pos = jax.random.randint(key_other, (), 0, WB - 1).astype(jnp.int32)
    last_pos = jnp.int32(WB - 1)
    coin_flip = jax.random.randint(key_coin, (), 0, 2).astype(jnp.int32)
    first_entry = coin_flip * last_pos + (1 - coin_flip) * other_pos
    second_entry = coin_flip * other_pos + (1 - coin_flip) * last_pos
    return jnp.stack([first_entry, second_entry]).astype(jnp.int32)


def block_levels(stream_key, dims, shards, smallest, largest):
    loudness, own = 1.0, jax.random.fold_in(stream_key, 6)
    for axis_at, parts in shards:
        steps = jnp.exp(jax.random.uniform(jax.random.fold_in(own, axis_at), (parts,), jnp.float32, smallest / len(shards), largest / len(shards)))
        loudness = loudness * jnp.repeat(steps, dims[axis_at] // parts).reshape([-1 if axis == axis_at else 1 for axis in range(len(dims))])
    return loudness


def bell_draw(rng, extent, width, most, shards=(), kind=jnp.bfloat16):
    array = width * jax.random.normal(rng, extent, jnp.float32)
    if shards:
        array = array * block_levels(rng, extent, shards, -0.22, 0.18)
    return jnp.clip(array, -most, most).astype(kind)


def setup_inputs(seed: int = 0) -> dict:
    arg_keys = jax.random.split(jax.random.key(seed), 9)
    return {
        "factor_rows": bell_draw(arg_keys[0], (WROWS, WROWS), WROWS ** -0.5, 0.0625, ((0, 16),)),
        "diag_inverse": draw_diag_inverse(jax.random.fold_in(arg_keys[8], 71), 0),
        "inducing": bell_draw(arg_keys[2], (DIM, WROWS), 1.0, 6.0, ((1, 16),), jnp.float32),
        "data_points": bell_draw(arg_keys[3], (DIM, NTOT), 1.0, 6.0, ((1, 8),), jnp.float32),
        "lengthscale": jnp.clip(jnp.exp(jax.random.uniform(arg_keys[4], (DIM,), jnp.float32, math.log(1.5), math.log(4.0))), 1.5, 4.0),
        "carried": bell_draw(arg_keys[5], (WROWS, NTOT), 0.5, 4.0, ((0, 16), (1, 8)), jnp.float32),
        "block_order": jax.random.permutation(arg_keys[6], WB).astype(jnp.int32),
        "panel_pair": draw_panel_pair(jax.random.fold_in(arg_keys[8], 71), 0),
    }


def reference(factor_rows, diag_inverse, inducing, data_points, lengthscale, carried, block_order, panel_pair):
    distance = jnp.zeros((WROWS, NTOT), jnp.float32)
    for feature in range(DIM):
        offset = (inducing[feature][:, None] - data_points[feature][None, :]) / lengthscale[feature]
        distance = distance + offset * offset
    kernel = jnp.exp(-0.5 * distance)
    residual = kernel - carried
    position = jnp.zeros((WB,), jnp.int32).at[block_order].set(jnp.arange(WB, dtype=jnp.int32))
    row_position = jnp.repeat(position, BLOCK)
    solved = jnp.zeros((WROWS, NTOT), jnp.bfloat16)

    def turn(index, carry):
        residual, solved = carry
        start = (block_order[index] * BLOCK).astype(jnp.int32)
        rows_now = lax.dynamic_slice_in_dim(residual, start, BLOCK, 0)
        inverse_now = lax.dynamic_slice_in_dim(diag_inverse, start, BLOCK, 0)
        panel_now = jnp.dot(inverse_now, rows_now, precision=lax.Precision.HIGHEST,
                            preferred_element_type=jnp.float32).astype(jnp.bfloat16)
        solved = lax.dynamic_update_slice_in_dim(solved, panel_now, start, 0)
        factor_cols = lax.dynamic_slice_in_dim(factor_rows, (index * BLOCK).astype(jnp.int32), BLOCK, 1)
        change = jnp.dot(factor_cols, panel_now, preferred_element_type=jnp.float32)
        residual = jnp.where((row_position > index)[:, None], residual - change, residual)
        return residual, solved

    residual, solved = lax.fori_loop(0, WB, turn, (residual, solved))
    first_tile = lax.dynamic_slice_in_dim(solved, (block_order[panel_pair[0]] * BLOCK).astype(jnp.int32), BLOCK, 0)
    second_tile = lax.dynamic_slice_in_dim(solved, (block_order[panel_pair[1]] * BLOCK).astype(jnp.int32), BLOCK, 0)
    stacked = jnp.concatenate([first_tile, second_tile], 0)
    product = jnp.dot(stacked, stacked.T, preferred_element_type=jnp.float32)
    gram = jnp.tril(product) * (1.0 / NTOT)
    return solved, gram
```

```python
import functools

import jax
import jax.numpy as jnp
from jax import lax
from jax.experimental import pallas as pl
from jax.experimental.pallas import tpu as pltpu
from jax.sharding import PartitionSpec as P

MESH = pl.DeviceIdType.MESH
NT = (((1,), (1,)), ((), ()))
TN = (((0,), (0,)), ((), ()))
f32 = jnp.float32
bf16 = jnp.bfloat16

NB, W, NODES, QUAD = 16, 512, 4, 4


def kernel(
    order, pair, scales, factor, dinv, ind_t, points, carried, solved_t, gram,
    stage, fact, ycur, y0t, cand, xall, fcrit, dbf, xq, solt, st, parts, inbox, piece, tile,
    n_sem, y_s, y_r, f_s, f_r, l_s, l_r, c_s, c_r, s_s, s_r, g_s, g_r, o_s, o_r,
):
    cols = points.shape[1]
    share = cols // QUAD
    half = share // 2
    dp = lax.axis_index("dp")
    me = lax.axis_index("ind")
    node = lax.div(me, QUAD)
    q = lax.rem(me, QUAD)
    core = lax.rem(q, 2)
    xlo = lax.div(q, 2)
    q1 = 2 * xlo + 1 - core
    q2 = 2 * (1 - xlo) + core
    q3 = 2 * (1 - xlo) + 1 - core
    base = node * QUAD
    up = lax.rem(node + 1, NODES) * QUAD + q
    down = lax.rem(node + NODES - 1, NODES) * QUAD + q
    other_dp = dp + 1 - 2 * lax.rem(dp, 2)
    rank = dp * QUAD + q
    ranks = 8 * QUAD

    def at(d, i):
        return {"dp": d, "ind": i}

    def remote(src, dst, ssem, rsem, dev):
        return pltpu.make_async_remote_copy(
            src_ref=src, dst_ref=dst, send_sem=ssem, recv_sem=rsem,
            device_id=dev, device_id_type=MESH,
        )

    def n_copy(b):
        return pltpu.make_async_copy(
            factor.at[:, pl.ds(pl.multiple_of(b * W, W), W)], stage.at[b], n_sem.at[b]
        )

    @pl.loop(0, NB - 1)
    def _(b):
        n_copy(b).start()

    barrier = pltpu.get_barrier_semaphore()

    @pl.loop(1, ranks)
    def _(k):
        t = lax.rem(rank + k, ranks)
        pl.semaphore_signal(
            barrier, inc=1, device_id=at(lax.div(t, QUAD), base + lax.rem(t, QUAD)), device_id_type=MESH
        )

    @pl.loop(0, NB - QUAD)
    def _(k):
        pl.semaphore_signal(
            barrier, inc=1, device_id=at(dp, lax.rem(base + QUAD + k, NB)), device_id_type=MESH
        )

    distance = jnp.zeros((W, cols), f32)
    for feature in range(points.shape[0]):
        inverse = jnp.full((1, 1), 1.0, f32) / scales[feature]
        offset = (ind_t[:, feature : feature + 1] - points[feature : feature + 1, :]) * inverse
        distance = distance + offset * offset
    residual = jnp.exp(-0.5 * distance) - carried[...]
    y0 = jnp.dot(dinv[...], residual, precision=lax.Precision.HIGHEST, preferred_element_type=f32)
    y0t[...] = y0.T
    dbf[...] = dinv[...].astype(bf16)

    pl.semaphore_wait(barrier, ranks - 1 + NB - QUAD)

    quad = (q2, q3, q1)

    def y_copy(k):
        to = quad[k]
        return remote(
            y0t.at[pl.ds(pl.multiple_of(to * share, share), share)], ycur.at[q],
            y_s.at[k], y_r.at[k], at(dp, base + to),
        )

    for k in range(3):
        y_copy(k).start()
    ycur[q] = y0t[pl.ds(pl.multiple_of(q * share, share), share), :]

    top, bottom = pl.ds(0, W // 2), pl.ds(W // 2, W // 2)

    def f_copies(b):
        return (
            remote(fact.at[b, q, top], fact.at[b, q, top], f_s.at[b, 0], f_r.at[b, 0], at(dp, base + q2)),
            remote(fact.at[b, q, bottom], fact.at[b, q, bottom], f_s.at[b, 1], f_r.at[b, 1], at(other_dp, base + q2)),
            remote(fact.at[b, q], fact.at[b, q], f_s.at[b, 2], f_r.at[b, 2], at(dp, base + q1)),
        )

    def relay(b):
        return remote(fact.at[b, q2], fact.at[b, q2], l_s.at[b], l_r.at[b], at(dp, base + q1))

    @pl.loop(0, NB - 1)
    def _(b):
        n_copy(b).wait()
        fact[b, q] = jnp.dot(dbf[...], stage[b], preferred_element_type=f32).astype(bf16)
        for copy in f_copies(b):
            copy.start()

    def c_first(b):
        return (
            remote(cand.at[b, 0], cand.at[b, 1], c_s.at[b, 0], c_r.at[b, 0], at(dp, up)),
            remote(cand.at[b, 0], cand.at[b, 2], c_s.at[b, 1], c_r.at[b, 1], at(dp, down)),
        )

    lo, hi = pl.ds(0, half), pl.ds(half, half)

    def c_second(b):
        return (
            remote(cand.at[b, 1, lo], cand.at[b, 3, lo], c_s.at[b, 2], c_r.at[b, 2], at(dp, up)),
            remote(cand.at[b, 2, hi], cand.at[b, 3, hi], c_s.at[b, 3], c_r.at[b, 3], at(dp, down)),
        )

    def offer(b, value):
        cand[b, 0] = value.astype(bf16)
        for copy in c_first(b):
            copy.start()

    def pass_on(b):
        for got, on in zip(c_first(b), c_second(b)):
            got.wait_recv()
            on.start()

    def choose(b):
        for got in c_second(b):
            got.wait_recv()
        away = lax.rem(lax.div(order[b], QUAD) - node + NODES, NODES)
        x = jnp.where(
            away == 0, cand[b, 0],
            jnp.where(away == 3, cand[b, 1], jnp.where(away == 1, cand[b, 2], cand[b, 3])),
        )
        xall[b] = x
        return x

    for k in range(3):
        y_copy(k).wait_recv()
    offer(0, ycur[lax.rem(order[0], QUAD)])

    @pl.loop(0, NB - 1)
    def _(b):
        from_a, from_b, from_core = f_copies(b)
        from_a.wait_recv()
        from_b.wait_recv()
        relay(b).start()
        pass_on(b)
        from_core.wait_recv()
        relay(b).wait_recv()
        following = lax.rem(order[b + 1], QUAD)
        fcrit[...] = jnp.where(
            following == 0, fact[b, 0],
            jnp.where(following == 1, fact[b, 1], jnp.where(following == 2, fact[b, 2], fact[b, 3])),
        )
        x = choose(b)
        offer(b + 1, ycur[following] - lax.dot_general(x, fcrit[...], NT, preferred_element_type=f32))
        for j in range(QUAD):
            ycur[j] = ycur[j] - lax.dot_general(x, fact[b, j], NT, preferred_element_type=f32)

    pass_on(NB - 1)
    choose(NB - 1)

    st[:, :W] = xall[pair[0]]
    st[:, W:] = xall[pair[1]]
    wide = gram.shape[1] // NODES
    tall = parts.shape[0] // ranks
    my_cols = pl.ds(pl.multiple_of(node * wide, wide), wide)
    parts[...] = lax.dot_general(st[...], st[:, my_cols], TN, preferred_element_type=f32).astype(bf16)

    def g_copy(k):
        t = lax.rem(rank + k, ranks)
        return remote(
            parts.at[pl.ds(pl.multiple_of(t * tall, tall), tall)], inbox.at[k - 1],
            g_s.at[k - 1], g_r.at[k - 1], at(lax.div(t, QUAD), base + lax.rem(t, QUAD)),
        )

    @pl.loop(1, ranks)
    def _(k):
        g_copy(k).start()

    for j in range(QUAD):
        place = jnp.int32(0)
        for b in range(NB):
            place = jnp.where(order[b] == base + j, b, place)
        xq[j] = xall[place]
    mine = pl.ds(pl.multiple_of(q * share, share), share)

    def s_copy(k):
        return remote(xq.at[quad[k]], solt.at[mine], s_s.at[k], s_r.at[k], at(dp, base + quad[k]))

    for k in range(3):
        s_copy(k).start()
    solt[mine, :] = xq[q]

    total = parts[pl.ds(pl.multiple_of(rank * tall, tall), tall), :].astype(f32)

    def add(k, total):
        g_copy(k).wait_recv()
        return total + inbox[k - 1].astype(f32)

    total = lax.fori_loop(1, ranks, add, total)
    row = rank * tall + lax.broadcasted_iota(jnp.int32, (tall, wide), 0)
    col = node * wide + lax.broadcasted_iota(jnp.int32, (tall, wide), 1)
    scale = 1.0 / (cols * 8)
    result = jnp.where(row >= col, total * scale, 0.0).astype(bf16)
    piece[...] = result
    my_rows = pl.ds(pl.multiple_of(q * tall, tall), tall)

    def o_copy(k):
        return remote(
            piece, tile.at[my_rows, my_cols], o_s.at[k - 1], o_r.at[k - 1], at(dp, lax.rem(me + k, NB))
        )

    @pl.loop(1, NB)
    def _(k):
        o_copy(k).start()

    tile[my_rows, my_cols] = result

    for k in range(3):
        s_copy(k).wait_recv()
    solved_t[...] = solt[...]

    @pl.loop(0, NB - 1)
    def _(b):
        for copy in f_copies(b):
            copy.wait_send()
        relay(b).wait_send()

    @pl.loop(0, NB)
    def _(b):
        for copy in c_first(b) + c_second(b):
            copy.wait_send()

    for k in range(3):
        y_copy(k).wait_send()
        s_copy(k).wait_send()

    @pl.loop(1, ranks)
    def _(k):
        g_copy(k).wait_send()

    @pl.loop(1, NB)
    def _(k):
        o_copy(k).wait()

    gram[...] = tile[...]


def on_device(factor_rows, diag_inverse, inducing, data_points, lengthscale, carried, block_order, panel_pair):
    cols = data_points.shape[1]
    share = cols // QUAD
    ranks = 8 * QUAD
    side = 2 * W
    smem = pl.BlockSpec(memory_space=pltpu.SMEM)
    vmem = pl.BlockSpec(memory_space=pltpu.VMEM)
    dma = pltpu.SemaphoreType.DMA
    solved_t, gram = pl.pallas_call(
        kernel,
        out_shape=(
            jax.ShapeDtypeStruct((cols, W), bf16),
            jax.ShapeDtypeStruct((side // 8, side), bf16),
        ),
        in_specs=[smem, smem, smem, pl.BlockSpec(memory_space=pl.ANY), vmem, vmem, vmem, vmem],
        out_specs=(vmem, vmem),
        scratch_shapes=[
            pltpu.VMEM((NB - 1, W, W), bf16),
            pltpu.VMEM((NB - 1, QUAD, W, W), bf16),
            pltpu.VMEM((QUAD, share, W), f32),
            pltpu.VMEM((cols, W), f32),
            pltpu.VMEM((NB, NODES, share, W), bf16),
            pltpu.VMEM((NB, share, W), bf16),
            pltpu.VMEM((W, W), bf16),
            pltpu.VMEM((W, W), bf16),
            pltpu.VMEM((QUAD, share, W), bf16),
            pltpu.VMEM((cols, W), bf16),
            pltpu.VMEM((share, side), bf16),
            pltpu.VMEM((side, side // NODES), bf16),
            pltpu.VMEM((ranks - 1, side // ranks, side // NODES), bf16),
            pltpu.VMEM((side // ranks, side // NODES), bf16),
            pltpu.VMEM((side // 8, side), bf16),
            dma((NB - 1,)),
            dma((3,)), dma((3,)),
            dma((NB - 1, 3)), dma((NB - 1, 3)),
            dma((NB - 1,)), dma((NB - 1,)),
            dma((NB, 4)), dma((NB, 4)),
            dma((3,)), dma((3,)),
            dma((ranks - 1,)), dma((ranks - 1,)),
            dma((NB - 1,)), dma((NB - 1,)),
        ],
        compiler_params=pltpu.CompilerParams(
            collective_id=0, has_side_effects=True, vmem_limit_bytes=60 * 1024 * 1024
        ),
        name="substitute",
    )(block_order, panel_pair, lengthscale, factor_rows, diag_inverse, inducing.T, data_points, carried)
    return solved_t.T, gram.astype(f32)


def solution(mesh):
    in_specs = (
        P("ind", None),
        P("ind", None),
        P(None, "ind"),
        P(None, "dp"),
        P(),
        P("ind", "dp"),
        P(),
        P(),
    )
    out_specs = (P("ind", "dp"), P("dp", None))
    return jax.shard_map(
        on_device, mesh=mesh, in_specs=in_specs, out_specs=out_specs, check_vma=False
    )
```

```python
import functools

import jax
import jax.numpy as jnp
from jax import lax
from jax.experimental import pallas as pl
from jax.experimental.pallas import tpu as pltpu
from jax.sharding import PartitionSpec as P

MESH = pl.DeviceIdType.MESH
NT = (((1,), (1,)), ((), ()))
TN = (((0,), (0,)), ((), ()))
f32 = jnp.float32
bf16 = jnp.bfloat16

NB, W, NODES, QUAD = 16, 512, 4, 4


def kernel(
    order, pair, scales, factor, dinv, ind_t, points, carried, solved_t, gram,
    stage, fact, ycur, yin, y0t, cand, xall, fcrit, dbf, xq, solt, st, parts, inbox, piece, tile,
    n_sem, y_s, y_r, f_s, f_r, l_s, l_r, z_s, z_r, c_s, c_r, s_s, s_r, g_s, g_r, o_s, o_r,
):
    cols = points.shape[1]
    share = cols // QUAD
    dp = lax.axis_index("dp")
    me = lax.axis_index("ind")
    node = lax.div(me, QUAD)
    q = lax.rem(me, QUAD)
    core = lax.rem(q, 2)
    xlo = lax.div(q, 2)
    q1 = 2 * xlo + 1 - core
    q2 = 2 * (1 - xlo) + core
    q3 = 2 * (1 - xlo) + 1 - core
    base = node * QUAD
    up = lax.rem(node + 1, NODES) * QUAD + q
    down = lax.rem(node + NODES - 1, NODES) * QUAD + q
    across = lax.rem(node + 2, NODES) * QUAD + q
    other_dp = dp + 1 - 2 * lax.rem(dp, 2)
    z_next = lax.rem(dp + 2, 8)
    z_last = lax.rem(dp + 6, 8)
    parity = lax.rem(lax.div(dp, 2), 2)
    rank = dp * QUAD + q
    ranks = 8 * QUAD

    def at(d, i):
        return {"dp": d, "ind": i}

    def remote(src, dst, ssem, rsem, dev):
        return pltpu.make_async_remote_copy(
            src_ref=src, dst_ref=dst, send_sem=ssem, recv_sem=rsem,
            device_id=dev, device_id_type=MESH,
        )

    def n_copy(b):
        return pltpu.make_async_copy(
            factor.at[:, pl.ds(pl.multiple_of(b * W, W), W)], stage.at[b], n_sem.at[b]
        )

    @pl.loop(0, NB - 1)
    def _(b):
        n_copy(b).start()

    barrier = pltpu.get_barrier_semaphore()

    @pl.loop(1, ranks)
    def _(k):
        t = lax.rem(rank + k, ranks)
        pl.semaphore_signal(
            barrier, inc=1, device_id=at(lax.div(t, QUAD), base + lax.rem(t, QUAD)), device_id_type=MESH
        )

    @pl.loop(0, NB - QUAD)
    def _(k):
        pl.semaphore_signal(
            barrier, inc=1, device_id=at(dp, lax.rem(base + QUAD + k, NB)), device_id_type=MESH
        )

    distance = jnp.zeros((W, cols), f32)
    for feature in range(points.shape[0]):
        inverse = jnp.full((1, 1), 1.0, f32) / scales[feature]
        offset = (ind_t[:, feature : feature + 1] - points[feature : feature + 1, :]) * inverse
        distance = distance + offset * offset
    residual = jnp.exp(-0.5 * distance) - carried[...]
    y0 = jnp.dot(dinv[...], residual, precision=lax.Precision.HIGHEST, preferred_element_type=f32)
    y0 = y0.T
    y0t[...] = y0.astype(bf16)
    dbf[...] = dinv[...].astype(bf16)

    pl.semaphore_wait(barrier, ranks - 1 + NB - QUAD)

    quad = (q2, q3, q1)

    def y_copy(k):
        to = quad[k]
        return remote(
            y0t.at[pl.ds(pl.multiple_of(to * share, share), share)], yin.at[q],
            y_s.at[k], y_r.at[k], at(dp, base + to),
        )

    for k in range(3):
        y_copy(k).start()
    ycur[q] = y0t[pl.ds(pl.multiple_of(q * share, share), share), :].astype(f32)

    part = W // 4
    q_a = pl.ds(pl.multiple_of(2 * parity * part, part), part)
    q_b = pl.ds(pl.multiple_of((2 * parity + 1) * part, part), part)

    def f_copies(b):
        return (
            remote(fact.at[b, q, q_a], fact.at[b, q, q_a], f_s.at[b, 0], f_r.at[b, 0], at(dp, base + q2)),
            remote(fact.at[b, q, q_b], fact.at[b, q, q_b], f_s.at[b, 1], f_r.at[b, 1], at(other_dp, base + q2)),
            remote(fact.at[b, q], fact.at[b, q], f_s.at[b, 2], f_r.at[b, 2], at(dp, base + q1)),
        )

    def z_copies(b):
        return (
            remote(fact.at[b, q2, q_a], fact.at[b, q2, q_a], z_s.at[b, 0], z_r.at[b, 0], at(z_last, me)),
            remote(fact.at[b, q2, q_b], fact.at[b, q2, q_b], z_s.at[b, 1], z_r.at[b, 1], at(z_next, me)),
        )

    def relay(b):
        return remote(fact.at[b, q2], fact.at[b, q2], l_s.at[b], l_r.at[b], at(dp, base + q1))

    def share_z(b):
        for got, on in zip(f_copies(b), z_copies(b)):
            got.wait_recv()
            on.start()

    def share_core(b):
        for got in z_copies(b):
            got.wait_recv()
        relay(b).start()

    @pl.loop(0, NB - 1)
    def _(b):
        n_copy(b).wait()
        fact[b, q] = jnp.dot(dbf[...], stage[b], preferred_element_type=f32).astype(bf16)
        for copy in f_copies(b):
            copy.start()

    def c_copies(b):
        return (
            remote(cand.at[b, 0], cand.at[b, 3], c_s.at[b, 2], c_r.at[b, 2], at(dp, across)),
            remote(cand.at[b, 0], cand.at[b, 1], c_s.at[b, 0], c_r.at[b, 0], at(dp, up)),
            remote(cand.at[b, 0], cand.at[b, 2], c_s.at[b, 1], c_r.at[b, 1], at(dp, down)),
        )


    def offer(b, value):
        cand[b, 0] = value.astype(bf16)
        for copy in c_copies(b):
            copy.start()

    def choose(b):
        for got in c_copies(b):
            got.wait_recv()
        away = lax.rem(lax.div(order[b], QUAD) - node + NODES, NODES)
        x = jnp.where(
            away == 0, cand[b, 0],
            jnp.where(away == 3, cand[b, 1], jnp.where(away == 1, cand[b, 2], cand[b, 3])),
        )
        xall[b] = x
        return x

    share_z(0)
    for k in range(3):
        y_copy(k).wait_recv()
        ycur[quad[k]] = yin[quad[k]].astype(f32)
    offer(0, ycur[lax.rem(order[0], QUAD)])
    share_core(0)
    share_z(1)

    @pl.loop(0, NB - 1)
    def _(b):
        @pl.when(b + 1 < NB - 1)
        def _():
            share_core(b + 1)

        @pl.when(b + 2 < NB - 1)
        def _():
            share_z(b + 2)

        f_copies(b)[2].wait_recv()
        relay(b).wait_recv()
        following = lax.rem(order[b + 1], QUAD)
        fcrit[...] = jnp.where(
            following == 0, fact[b, 0],
            jnp.where(following == 1, fact[b, 1], jnp.where(following == 2, fact[b, 2], fact[b, 3])),
        )
        x = choose(b)
        offer(b + 1, ycur[following] - lax.dot_general(x, fcrit[...], NT, preferred_element_type=f32))
        for j in range(QUAD):
            ycur[j] = ycur[j] - lax.dot_general(x, fact[b, j], NT, preferred_element_type=f32)

    choose(NB - 1)

    st[:, :W] = xall[pair[0]]
    st[:, W:] = xall[pair[1]]
    wide = gram.shape[1] // NODES
    tall = parts.shape[0] // ranks
    my_cols = pl.ds(pl.multiple_of(node * wide, wide), wide)
    parts[...] = lax.dot_general(st[...], st[:, my_cols], TN, preferred_element_type=f32).astype(bf16)

    def g_copy(k):
        t = lax.rem(rank + k, ranks)
        return remote(
            parts.at[pl.ds(pl.multiple_of(t * tall, tall), tall)], inbox.at[k - 1],
            g_s.at[k - 1], g_r.at[k - 1], at(lax.div(t, QUAD), base + lax.rem(t, QUAD)),
        )

    @pl.loop(1, ranks)
    def _(k):
        g_copy(k).start()

    for j in range(QUAD):
        place = jnp.int32(0)
        for b in range(NB):
            place = jnp.where(order[b] == base + j, b, place)
        xq[j] = xall[place]
    mine = pl.ds(pl.multiple_of(q * share, share), share)

    def s_copy(k):
        return remote(xq.at[quad[k]], solt.at[mine], s_s.at[k], s_r.at[k], at(dp, base + quad[k]))

    for k in range(3):
        s_copy(k).start()
    solt[mine, :] = xq[q]

    total = parts[pl.ds(pl.multiple_of(rank * tall, tall), tall), :].astype(f32)

    def add(k, total):
        g_copy(k).wait_recv()
        return total + inbox[k - 1].astype(f32)

    total = lax.fori_loop(1, ranks, add, total)
    row = rank * tall + lax.broadcasted_iota(jnp.int32, (tall, wide), 0)
    col = node * wide + lax.broadcasted_iota(jnp.int32, (tall, wide), 1)
    scale = 1.0 / (cols * 8)
    result = jnp.where(row >= col, total * scale, 0.0).astype(bf16)
    piece[...] = result
    my_rows = pl.ds(pl.multiple_of(q * tall, tall), tall)

    def o_copy(k):
        return remote(
            piece, tile.at[my_rows, my_cols], o_s.at[k - 1], o_r.at[k - 1], at(dp, lax.rem(me + k, NB))
        )

    @pl.loop(1, NB)
    def _(k):
        o_copy(k).start()

    tile[my_rows, my_cols] = result

    for k in range(3):
        s_copy(k).wait_recv()
    solved_t[...] = solt[...]

    @pl.loop(0, NB - 1)
    def _(b):
        for copy in f_copies(b) + z_copies(b):
            copy.wait_send()
        relay(b).wait_send()

    @pl.loop(0, NB)
    def _(b):
        for copy in c_copies(b):
            copy.wait_send()

    for k in range(3):
        y_copy(k).wait_send()
        s_copy(k).wait_send()

    @pl.loop(1, ranks)
    def _(k):
        g_copy(k).wait_send()

    @pl.loop(1, NB)
    def _(k):
        o_copy(k).wait()

    gram[...] = tile[...]


def on_device(factor_rows, diag_inverse, inducing, data_points, lengthscale, carried, block_order, panel_pair):
    cols = data_points.shape[1]
    share = cols // QUAD
    ranks = 8 * QUAD
    side = 2 * W
    smem = pl.BlockSpec(memory_space=pltpu.SMEM)
    vmem = pl.BlockSpec(memory_space=pltpu.VMEM)
    dma = pltpu.SemaphoreType.DMA
    solved_t, gram = pl.pallas_call(
        kernel,
        out_shape=(
            jax.ShapeDtypeStruct((cols, W), bf16),
            jax.ShapeDtypeStruct((side // 8, side), bf16),
        ),
        in_specs=[smem, smem, smem, pl.BlockSpec(memory_space=pl.ANY), vmem, vmem, vmem, vmem],
        out_specs=(vmem, vmem),
        scratch_shapes=[
            pltpu.VMEM((NB - 1, W, W), bf16),
            pltpu.VMEM((NB - 1, QUAD, W, W), bf16),
            pltpu.VMEM((QUAD, share, W), f32),
            pltpu.VMEM((QUAD, share, W), bf16),
            pltpu.VMEM((cols, W), bf16),
            pltpu.VMEM((NB, NODES, share, W), bf16),
            pltpu.VMEM((NB, share, W), bf16),
            pltpu.VMEM((W, W), bf16),
            pltpu.VMEM((W, W), bf16),
            pltpu.VMEM((QUAD, share, W), bf16),
            pltpu.VMEM((cols, W), bf16),
            pltpu.VMEM((share, side), bf16),
            pltpu.VMEM((side, side // NODES), bf16),
            pltpu.VMEM((ranks - 1, side // ranks, side // NODES), bf16),
            pltpu.VMEM((side // ranks, side // NODES), bf16),
            pltpu.VMEM((side // 8, side), bf16),
            dma((NB - 1,)),
            dma((3,)), dma((3,)),
            dma((NB - 1, 3)), dma((NB - 1, 3)),
            dma((NB - 1,)), dma((NB - 1,)),
            dma((NB - 1, 2)), dma((NB - 1, 2)),
            dma((NB, 3)), dma((NB, 3)),
            dma((3,)), dma((3,)),
            dma((ranks - 1,)), dma((ranks - 1,)),
            dma((NB - 1,)), dma((NB - 1,)),
        ],
        compiler_params=pltpu.CompilerParams(
            collective_id=0, has_side_effects=True, vmem_limit_bytes=60 * 1024 * 1024
        ),
        name="substitute",
    )(block_order, panel_pair, lengthscale, factor_rows, diag_inverse, inducing.T, data_points, carried)
    return solved_t.T, gram.astype(f32)


def solution(mesh):
    in_specs = (
        P("ind", None),
        P("ind", None),
        P(None, "ind"),
        P(None, "dp"),
        P(),
        P("ind", "dp"),
        P(),
        P(),
    )
    out_specs = (P("ind", "dp"), P("dp", None))
    return jax.shard_map(
        on_device, mesh=mesh, in_specs=in_specs, out_specs=out_specs, check_vma=False
    )
```

```python
import functools

import jax
import jax.numpy as jnp
from jax import lax
from jax.experimental import pallas as pl
from jax.experimental.pallas import tpu as pltpu
from jax.sharding import PartitionSpec as P

MESH = pl.DeviceIdType.MESH
NT = (((1,), (1,)), ((), ()))
TN = (((0,), (0,)), ((), ()))
f32 = jnp.float32
bf16 = jnp.bfloat16

NB, W, NODES, QUAD = 16, 512, 4, 4
LEAD, ZLEAD, HALVES = 6, 3, 4


def kernel(
    order, pair, scales, factor, dinv, inducing, points, carried, solved_t, gram,
    stage, fact, ycur, yin, y0t, cand, xall, fcrit, dbf, xq, solt, st, parts, inbox, piece, tile,
    n_sem, y_s, y_r, f_s, f_r, l_s, l_r, z_s, z_r, c_s, c_r, s_s, s_r, g_s, g_r, o_s, o_r,
):
    cols = points.shape[1]
    share = cols // QUAD
    dp = lax.axis_index("dp")
    me = lax.axis_index("ind")
    node = lax.div(me, QUAD)
    q = lax.rem(me, QUAD)
    core = lax.rem(q, 2)
    xlo = lax.div(q, 2)
    q1 = 2 * xlo + 1 - core
    q2 = 2 * (1 - xlo) + core
    q3 = 2 * (1 - xlo) + 1 - core
    base = node * QUAD
    up = lax.rem(node + 1, NODES) * QUAD + q
    down = lax.rem(node + NODES - 1, NODES) * QUAD + q
    across = lax.rem(node + 2, NODES) * QUAD + q
    other_dp = dp + 1 - 2 * lax.rem(dp, 2)
    z_next = lax.rem(dp + 2, 8)
    z_last = lax.rem(dp + 6, 8)
    parity = lax.rem(lax.div(dp, 2), 2)
    rank = dp * QUAD + q
    ranks = 8 * QUAD

    def at(d, i):
        return {"dp": d, "ind": i}

    def remote(src, dst, ssem, rsem, dev):
        return pltpu.make_async_remote_copy(
            src_ref=src, dst_ref=dst, send_sem=ssem, recv_sem=rsem,
            device_id=dev, device_id_type=MESH,
        )

    def n_copy(b):
        return pltpu.make_async_copy(
            factor.at[:, pl.ds(pl.multiple_of(b * W, W), W)], stage.at[b], n_sem.at[b]
        )

    @pl.loop(0, NB - 1)
    def _(b):
        n_copy(b).start()

    barrier = pltpu.get_barrier_semaphore()

    @pl.loop(1, ranks)
    def _(k):
        t = lax.rem(rank + k, ranks)
        pl.semaphore_signal(
            barrier, inc=1, device_id=at(lax.div(t, QUAD), base + lax.rem(t, QUAD)), device_id_type=MESH
        )

    @pl.loop(0, NB - QUAD)
    def _(k):
        pl.semaphore_signal(
            barrier, inc=1, device_id=at(dp, lax.rem(base + QUAD + k, NB)), device_id_type=MESH
        )

    along = inducing[...].T
    distance = jnp.zeros((W, cols), f32)
    for feature in range(points.shape[0]):
        inverse = jnp.full((1, 1), 1.0, f32) / scales[feature]
        offset = (along[:, feature : feature + 1] - points[feature : feature + 1, :]) * inverse
        distance = distance + offset * offset
    residual = jnp.exp(-0.5 * distance) - carried[...]
    y0 = jnp.dot(dinv[...], residual, precision=lax.Precision.HIGHEST, preferred_element_type=f32)
    y0 = y0.T
    y0t[...] = y0.astype(bf16)
    dbf[...] = dinv[...].astype(bf16)

    pl.semaphore_wait(barrier, ranks - 1 + NB - QUAD)

    quad = (q2, q3, q1)

    def y_copy(k):
        to = quad[k]
        return remote(
            y0t.at[pl.ds(pl.multiple_of(to * share, share), share)], yin.at[q],
            y_s.at[k], y_r.at[k], at(dp, base + to),
        )

    for k in range(3):
        y_copy(k).start()
    ycur[q] = y0t[pl.ds(pl.multiple_of(q * share, share), share), :].astype(f32)

    part = W // 4
    q_a = pl.ds(pl.multiple_of(2 * parity * part, part), part)
    q_b = pl.ds(pl.multiple_of((2 * parity + 1) * part, part), part)

    def f_copies(b):
        return (
            remote(fact.at[b, q, q_a], fact.at[b, q, q_a], f_s.at[b, 0], f_r.at[b, 0], at(dp, base + q2)),
            remote(fact.at[b, q, q_b], fact.at[b, q, q_b], f_s.at[b, 1], f_r.at[b, 1], at(other_dp, base + q2)),
            remote(fact.at[b, q], fact.at[b, q], f_s.at[b, 2], f_r.at[b, 2], at(dp, base + q1)),
        )

    def z_copies(b):
        return (
            remote(fact.at[b, q2, q_a], fact.at[b, q2, q_a], z_s.at[b, 0], z_r.at[b, 0], at(z_last, me)),
            remote(fact.at[b, q2, q_b], fact.at[b, q2, q_b], z_s.at[b, 1], z_r.at[b, 1], at(z_next, me)),
        )

    def relay(b):
        return remote(fact.at[b, q2], fact.at[b, q2], l_s.at[b], l_r.at[b], at(dp, base + q1))

    def share_z(b):
        for got, on in zip(f_copies(b), z_copies(b)):
            got.wait_recv()
            on.start()

    def share_core(b):
        for got in z_copies(b):
            got.wait_recv()
        relay(b).start()

    def make(b):
        n_copy(b).wait()
        fact[b, q] = jnp.dot(dbf[...], stage[b], preferred_element_type=f32).astype(bf16)
        for copy in f_copies(b):
            copy.start()

    half = share // HALVES

    def c_copies(b, h):
        rows = pl.ds(h * half, half)
        return tuple(
            remote(cand.at[b, 0, rows], cand.at[b, n + 1, rows], c_s.at[b, h, n], c_r.at[b, h, n], at(dp, to))
            for n, to in ((2, across), (0, up), (1, down))
        )

    def offer(b, h, value):
        cand[b, 0, pl.ds(h * half, half)] = value.astype(bf16)
        for copy in c_copies(b, h):
            copy.start()

    def choose(b, h):
        rows = pl.ds(h * half, half)
        for got in c_copies(b, h):
            got.wait_recv()
        away = lax.rem(lax.div(order[b], QUAD) - node + NODES, NODES)
        x = jnp.where(
            away == 0, cand[b, 0, rows],
            jnp.where(away == 3, cand[b, 1, rows], jnp.where(away == 1, cand[b, 2, rows], cand[b, 3, rows])),
        )
        xall[b, rows] = x
        return x

    @pl.loop(0, LEAD)
    def _(b):
        make(b)

    share_z(0)
    for k in range(3):
        y_copy(k).wait_recv()
        ycur[quad[k]] = yin[quad[k]].astype(f32)
    first = lax.rem(order[0], QUAD)
    for h in range(HALVES):
        offer(0, h, ycur[first, pl.ds(h * half, half)])
    for b in range(1, ZLEAD):
        share_z(b)
    share_core(0)

    @pl.loop(0, NB - 1)
    def _(b):
        @pl.when(b + LEAD < NB - 1)
        def _():
            make(b + LEAD)

        @pl.when(b + ZLEAD < NB - 1)
        def _():
            share_z(b + ZLEAD)

        @pl.when(b + 1 < NB - 1)
        def _():
            share_core(b + 1)

        f_copies(b)[2].wait_recv()
        relay(b).wait_recv()
        following = lax.rem(order[b + 1], QUAD)
        fcrit[...] = jnp.where(
            following == 0, fact[b, 0],
            jnp.where(following == 1, fact[b, 1], jnp.where(following == 2, fact[b, 2], fact[b, 3])),
        )
        for h in range(HALVES):
            x = choose(b, h)
            known = ycur[following, pl.ds(h * half, half)]
            offer(b + 1, h, known - lax.dot_general(x, fcrit[...], NT, preferred_element_type=f32))
        for j in range(QUAD):
            ycur[j] = ycur[j] - lax.dot_general(xall[b], fact[b, j], NT, preferred_element_type=f32)

    for h in range(HALVES):
        choose(NB - 1, h)

    st[:, :W] = xall[pair[0]]
    st[:, W:] = xall[pair[1]]
    wide = gram.shape[1] // NODES
    tall = parts.shape[0] // ranks
    my_cols = pl.ds(pl.multiple_of(node * wide, wide), wide)
    parts[...] = lax.dot_general(st[...], st[:, my_cols], TN, preferred_element_type=f32).astype(bf16)

    def g_copy(k):
        t = lax.rem(rank + k, ranks)
        return remote(
            parts.at[pl.ds(pl.multiple_of(t * tall, tall), tall)], inbox.at[k - 1],
            g_s.at[k - 1], g_r.at[k - 1], at(lax.div(t, QUAD), base + lax.rem(t, QUAD)),
        )

    @pl.loop(1, ranks)
    def _(k):
        g_copy(k).start()

    for j in range(QUAD):
        place = jnp.int32(0)
        for b in range(NB):
            place = jnp.where(order[b] == base + j, b, place)
        xq[j] = xall[place]
    mine = pl.ds(pl.multiple_of(q * share, share), share)

    def s_copy(k):
        return remote(xq.at[quad[k]], solt.at[mine], s_s.at[k], s_r.at[k], at(dp, base + quad[k]))

    for k in range(3):
        s_copy(k).start()
    solt[mine, :] = xq[q]

    total = parts[pl.ds(pl.multiple_of(rank * tall, tall), tall), :].astype(f32)

    def add(k, total):
        g_copy(k).wait_recv()
        return total + inbox[k - 1].astype(f32)

    total = lax.fori_loop(1, ranks, add, total)
    row = rank * tall + lax.broadcasted_iota(jnp.int32, (tall, wide), 0)
    col = node * wide + lax.broadcasted_iota(jnp.int32, (tall, wide), 1)
    scale = 1.0 / (cols * 8)
    result = jnp.where(row >= col, total * scale, 0.0).astype(bf16)
    piece[...] = result
    my_rows = pl.ds(pl.multiple_of(q * tall, tall), tall)

    def o_copy(k):
        return remote(
            piece, tile.at[my_rows, my_cols], o_s.at[k - 1], o_r.at[k - 1], at(dp, lax.rem(me + k, NB))
        )

    @pl.loop(1, NB)
    def _(k):
        o_copy(k).start()

    tile[my_rows, my_cols] = result

    for k in range(3):
        s_copy(k).wait_recv()
    solved_t[...] = solt[...]

    @pl.loop(0, NB - 1)
    def _(b):
        for copy in f_copies(b) + z_copies(b):
            copy.wait_send()
        relay(b).wait_send()

    @pl.loop(0, NB)
    def _(b):
        for h in range(HALVES):
            for copy in c_copies(b, h):
                copy.wait_send()

    for k in range(3):
        y_copy(k).wait_send()
        s_copy(k).wait_send()

    @pl.loop(1, ranks)
    def _(k):
        g_copy(k).wait_send()

    @pl.loop(1, NB)
    def _(k):
        o_copy(k).wait()

    gram[...] = tile[...]


def on_device(factor_rows, diag_inverse, inducing, data_points, lengthscale, carried, block_order, panel_pair):
    cols = data_points.shape[1]
    share = cols // QUAD
    ranks = 8 * QUAD
    side = 2 * W
    smem = pl.BlockSpec(memory_space=pltpu.SMEM)
    vmem = pl.BlockSpec(memory_space=pltpu.VMEM)
    dma = pltpu.SemaphoreType.DMA
    solved_t, gram = pl.pallas_call(
        kernel,
        out_shape=(
            jax.ShapeDtypeStruct((cols, W), bf16),
            jax.ShapeDtypeStruct((side // 8, side), bf16),
        ),
        in_specs=[smem, smem, smem, pl.BlockSpec(memory_space=pl.ANY), vmem, vmem, vmem, vmem],
        out_specs=(vmem, vmem),
        scratch_shapes=[
            pltpu.VMEM((NB - 1, W, W), bf16),
            pltpu.VMEM((NB - 1, QUAD, W, W), bf16),
            pltpu.VMEM((QUAD, share, W), f32),
            pltpu.VMEM((QUAD, share, W), bf16),
            pltpu.VMEM((cols, W), bf16),
            pltpu.VMEM((NB, NODES, share, W), bf16),
            pltpu.VMEM((NB, share, W), bf16),
            pltpu.VMEM((W, W), bf16),
            pltpu.VMEM((W, W), bf16),
            pltpu.VMEM((QUAD, share, W), bf16),
            pltpu.VMEM((cols, W), bf16),
            pltpu.VMEM((share, side), bf16),
            pltpu.VMEM((side, side // NODES), bf16),
            pltpu.VMEM((ranks - 1, side // ranks, side // NODES), bf16),
            pltpu.VMEM((side // ranks, side // NODES), bf16),
            pltpu.VMEM((side // 8, side), bf16),
            dma((NB - 1,)),
            dma((3,)), dma((3,)),
            dma((NB - 1, 3)), dma((NB - 1, 3)),
            dma((NB - 1,)), dma((NB - 1,)),
            dma((NB - 1, 2)), dma((NB - 1, 2)),
            dma((NB, HALVES, 3)), dma((NB, HALVES, 3)),
            dma((3,)), dma((3,)),
            dma((ranks - 1,)), dma((ranks - 1,)),
            dma((NB - 1,)), dma((NB - 1,)),
        ],
        compiler_params=pltpu.CompilerParams(
            collective_id=0, has_side_effects=True, vmem_limit_bytes=60 * 1024 * 1024
        ),
        name="substitute",
    )(block_order, panel_pair, lengthscale, factor_rows, diag_inverse, inducing, data_points, carried)
    return solved_t.T, gram.astype(f32)


def solution(mesh):
    in_specs = (
        P("ind", None),
        P("ind", None),
        P(None, "ind"),
        P(None, "dp"),
        P(),
        P("ind", "dp"),
        P(),
        P(),
    )
    out_specs = (P("ind", "dp"), P("dp", None))
    return jax.shard_map(
        on_device, mesh=mesh, in_specs=in_specs, out_specs=out_specs, check_vma=False
    )
```

```python
import functools

import jax
import jax.numpy as jnp
from jax import lax
from jax.experimental import pallas as pl
from jax.experimental.pallas import tpu as pltpu
from jax.sharding import PartitionSpec as P

MESH = pl.DeviceIdType.MESH
NT = (((1,), (1,)), ((), ()))
TN = (((0,), (0,)), ((), ()))
f32 = jnp.float32
bf16 = jnp.bfloat16

NB, W, NODES, QUAD = 16, 512, 4, 4
SOON, LEAD, HALVES = 3, 6, 4


def kernel(
    order, pair, scales, factor, inverse_hbm, carried_hbm, inducing, points, solved_t, gram,
    dinv, carried, stage, fact, ycur, yin, y0t, cand, xall, fcrit, dbf, xq, solt, st, parts, inbox, piece, tile,
    i_sem, n_sem, y_s, y_r, f_s, f_r, l_s, l_r, z_s, z_r, c_s, c_r, s_s, s_r, g_s, g_r, o_s, o_r,
):
    cols = points.shape[1]
    share = cols // QUAD
    dp = lax.axis_index("dp")
    me = lax.axis_index("ind")
    node = lax.div(me, QUAD)
    q = lax.rem(me, QUAD)
    core = lax.rem(q, 2)
    xlo = lax.div(q, 2)
    q1 = 2 * xlo + 1 - core
    q2 = 2 * (1 - xlo) + core
    q3 = 2 * (1 - xlo) + 1 - core
    base = node * QUAD
    up = lax.rem(node + 1, NODES) * QUAD + q
    down = lax.rem(node + NODES - 1, NODES) * QUAD + q
    across = lax.rem(node + 2, NODES) * QUAD + q
    other_dp = dp + 1 - 2 * lax.rem(dp, 2)
    z_next = lax.rem(dp + 2, 8)
    z_last = lax.rem(dp + 6, 8)
    parity = lax.rem(lax.div(dp, 2), 2)
    rank = dp * QUAD + q
    ranks = 8 * QUAD

    def at(d, i):
        return {"dp": d, "ind": i}

    def remote(src, dst, ssem, rsem, dev):
        return pltpu.make_async_remote_copy(
            src_ref=src, dst_ref=dst, send_sem=ssem, recv_sem=rsem,
            device_id=dev, device_id_type=MESH,
        )

    def n_copy(b):
        return pltpu.make_async_copy(
            factor.at[:, pl.ds(pl.multiple_of(b * W, W), W)], stage.at[b], n_sem.at[b]
        )

    d_copy = pltpu.make_async_copy(inverse_hbm, dinv, i_sem.at[0])
    r_copy = pltpu.make_async_copy(carried_hbm, carried, i_sem.at[1])
    d_copy.start()
    n_copy(0).start()
    r_copy.start()

    @pl.loop(1, NB - 1)
    def _(b):
        n_copy(b).start()

    barrier = pltpu.get_barrier_semaphore()
    near = (
        at(dp, up), at(dp, down), at(dp, across), at(dp, base + q2), at(other_dp, base + q2),
        at(z_next, me), at(z_last, me), at(dp, base + q3), at(dp, base + q1),
    )
    for device in near:
        pl.semaphore_signal(barrier, inc=1, device_id=device, device_id_type=MESH)

    def compute(b):
        n_copy(b).wait()
        fact[b, q] = jnp.dot(dbf[...], stage[b], preferred_element_type=f32).astype(bf16)

    d_copy.wait()
    dbf[...] = dinv[...].astype(bf16)
    compute(0)

    along = inducing[...].T
    distance = jnp.zeros((W, cols), f32)
    for feature in range(points.shape[0]):
        inverse = jnp.full((1, 1), 1.0, f32) / scales[feature]
        offset = (along[:, feature : feature + 1] - points[feature : feature + 1, :]) * inverse
        distance = distance + offset * offset
    r_copy.wait()
    residual = jnp.exp(-0.5 * distance) - carried[...]
    y0 = jnp.dot(dinv[...], residual, precision=lax.Precision.HIGHEST, preferred_element_type=f32)
    y0 = y0.T
    y0t[...] = y0.astype(bf16)

    pl.semaphore_wait(barrier, len(near))

    quad = (q2, q3, q1)

    def y_copy(k):
        to = quad[k]
        return remote(
            y0t.at[pl.ds(pl.multiple_of(to * share, share), share)], yin.at[q],
            y_s.at[k], y_r.at[k], at(dp, base + to),
        )


    part = W // 4
    q_a = pl.ds(pl.multiple_of(2 * parity * part, part), part)
    q_b = pl.ds(pl.multiple_of((2 * parity + 1) * part, part), part)

    def f_copies(b):
        return (
            remote(fact.at[b, q, q_a], fact.at[b, q, q_a], f_s.at[b, 0], f_r.at[b, 0], at(dp, base + q2)),
            remote(fact.at[b, q, q_b], fact.at[b, q, q_b], f_s.at[b, 1], f_r.at[b, 1], at(other_dp, base + q2)),
            remote(fact.at[b, q], fact.at[b, q], f_s.at[b, 2], f_r.at[b, 2], at(dp, base + q1)),
        )

    def z_copies(b):
        return (
            remote(fact.at[b, q2, q_a], fact.at[b, q2, q_a], z_s.at[b, 0], z_r.at[b, 0], at(z_last, me)),
            remote(fact.at[b, q2, q_b], fact.at[b, q2, q_b], z_s.at[b, 1], z_r.at[b, 1], at(z_next, me)),
        )

    def relay(b):
        return remote(fact.at[b, q2], fact.at[b, q2], l_s.at[b], l_r.at[b], at(dp, base + q1))

    def share_z(b):
        for got, on in zip(f_copies(b), z_copies(b)):
            got.wait_recv()
            on.start()

    def share_core(b):
        for got in z_copies(b):
            got.wait_recv()
        relay(b).start()

    def send(b):
        for copy in f_copies(b):
            copy.start()

    def make(b):
        compute(b)
        send(b)

    half = share // HALVES

    def c_copies(b, h):
        rows = pl.ds(h * half, half)
        return tuple(
            remote(cand.at[b, 0, rows], cand.at[b, n + 1, rows], c_s.at[b, h, n], c_r.at[b, h, n], at(dp, to))
            for n, to in ((2, across), (0, up), (1, down))
        )

    def offer(b, h, value):
        cand[b, 0, pl.ds(h * half, half)] = value.astype(bf16)
        for copy in c_copies(b, h):
            copy.start()

    def choose(b, h):
        rows = pl.ds(h * half, half)
        for got in c_copies(b, h):
            got.wait_recv()
        away = lax.rem(lax.div(order[b], QUAD) - node + NODES, NODES)
        x = jnp.where(
            away == 0, cand[b, 0, rows],
            jnp.where(away == 3, cand[b, 1, rows], jnp.where(away == 1, cand[b, 2, rows], cand[b, 3, rows])),
        )
        xall[b, rows] = x
        return x

    send(0)
    for k in range(3):
        y_copy(k).start()
    ycur[q] = y0t[pl.ds(pl.multiple_of(q * share, share), share), :].astype(f32)

    @pl.loop(1, SOON)
    def _(b):
        make(b)

    share_z(0)
    for k in range(3):
        y_copy(k).wait_recv()
        ycur[quad[k]] = yin[quad[k]].astype(f32)
    first = lax.rem(order[0], QUAD)
    for h in range(HALVES):
        offer(0, h, ycur[first, pl.ds(h * half, half)])

    @pl.loop(SOON, LEAD)
    def _(b):
        make(b)

    share_core(0)
    share_z(1)
    early = {
        1: ((share_z, 2), (share_core, 1)),
        2: ((share_z, 3), (share_core, 2), (share_z, 4)),
        3: ((share_core, 3), (share_z, 5), (share_core, 4), (share_z, 6)),
    }

    @pl.loop(0, NB - 1)
    def _(b):
        for step, work in early.items():
            @pl.when(b == step)
            def _():
                for share, block in work:
                    share(block)

        @pl.when((b > max(early)) & (b + 3 < NB - 1))
        def _():
            share_z(b + 3)

        @pl.when((b > max(early)) & (b + 1 < NB - 1))
        def _():
            share_core(b + 1)

        f_copies(b)[2].wait_recv()
        relay(b).wait_recv()
        following = lax.rem(order[b + 1], QUAD)
        fcrit[...] = jnp.where(
            following == 0, fact[b, 0],
            jnp.where(following == 1, fact[b, 1], jnp.where(following == 2, fact[b, 2], fact[b, 3])),
        )
        for h in range(HALVES):
            x = choose(b, h)
            known = ycur[following, pl.ds(h * half, half)]
            offer(b + 1, h, known - lax.dot_general(x, fcrit[...], NT, preferred_element_type=f32))
        for j in range(QUAD):
            ycur[j] = ycur[j] - lax.dot_general(xall[b], fact[b, j], NT, preferred_element_type=f32)

        @pl.when(b + LEAD < NB - 1)
        def _():
            make(b + LEAD)

    for h in range(HALVES):
        choose(NB - 1, h)

    st[:, :W] = xall[pair[0]]
    st[:, W:] = xall[pair[1]]
    wide = gram.shape[1] // NODES
    tall = parts.shape[0] // ranks
    my_cols = pl.ds(pl.multiple_of(node * wide, wide), wide)
    parts[...] = lax.dot_general(st[...], st[:, my_cols], TN, preferred_element_type=f32).astype(bf16)

    def g_copy(k):
        t = lax.rem(rank + k, ranks)
        return remote(
            parts.at[pl.ds(pl.multiple_of(t * tall, tall), tall)], inbox.at[k - 1],
            g_s.at[k - 1], g_r.at[k - 1], at(lax.div(t, QUAD), base + lax.rem(t, QUAD)),
        )

    @pl.loop(1, ranks)
    def _(k):
        g_copy(k).start()

    for j in range(QUAD):
        place = jnp.int32(0)
        for b in range(NB):
            place = jnp.where(order[b] == base + j, b, place)
        xq[j] = xall[place]
    mine = pl.ds(pl.multiple_of(q * share, share), share)

    def s_copy(k):
        return remote(xq.at[quad[k]], solt.at[mine], s_s.at[k], s_r.at[k], at(dp, base + quad[k]))

    for k in range(3):
        s_copy(k).start()
    solt[mine, :] = xq[q]

    total = parts[pl.ds(pl.multiple_of(rank * tall, tall), tall), :].astype(f32)

    def add(k, total):
        g_copy(k).wait_recv()
        return total + inbox[k - 1].astype(f32)

    total = lax.fori_loop(1, ranks, add, total)
    row = rank * tall + lax.broadcasted_iota(jnp.int32, (tall, wide), 0)
    col = node * wide + lax.broadcasted_iota(jnp.int32, (tall, wide), 1)
    scale = 1.0 / (cols * 8)
    result = jnp.where(row >= col, total * scale, 0.0).astype(bf16)
    piece[...] = result
    my_rows = pl.ds(pl.multiple_of(q * tall, tall), tall)

    def o_copy(k):
        return remote(
            piece, tile.at[my_rows, my_cols], o_s.at[k - 1], o_r.at[k - 1], at(dp, lax.rem(me + k, NB))
        )

    @pl.loop(1, NB)
    def _(k):
        o_copy(k).start()

    tile[my_rows, my_cols] = result

    for k in range(3):
        s_copy(k).wait_recv()
    solved_t[...] = solt[...]

    @pl.loop(0, NB - 1)
    def _(b):
        for copy in f_copies(b) + z_copies(b):
            copy.wait_send()
        relay(b).wait_send()

    @pl.loop(0, NB)
    def _(b):
        for h in range(HALVES):
            for copy in c_copies(b, h):
                copy.wait_send()

    for k in range(3):
        y_copy(k).wait_send()
        s_copy(k).wait_send()

    @pl.loop(1, ranks)
    def _(k):
        g_copy(k).wait_send()

    @pl.loop(1, NB)
    def _(k):
        o_copy(k).wait()

    gram[...] = tile[...]


def finish(solved_t, gram):
    def body(solved_t, gram, solved, gram_out):
        solved[...] = solved_t[...].T
        gram_out[...] = gram[...].astype(f32)

    cols, rows = solved_t.shape
    return pl.pallas_call(
        body,
        out_shape=(jax.ShapeDtypeStruct((rows, cols), bf16), jax.ShapeDtypeStruct(gram.shape, f32)),
        name="finish",
    )(solved_t, gram)


def on_device(factor_rows, diag_inverse, inducing, data_points, lengthscale, carried, block_order, panel_pair):
    cols = data_points.shape[1]
    share = cols // QUAD
    ranks = 8 * QUAD
    side = 2 * W
    smem = pl.BlockSpec(memory_space=pltpu.SMEM)
    vmem = pl.BlockSpec(memory_space=pltpu.VMEM)
    hbm = pl.BlockSpec(memory_space=pl.ANY)
    dma = pltpu.SemaphoreType.DMA
    solved_t, gram = pl.pallas_call(
        kernel,
        out_shape=(
            jax.ShapeDtypeStruct((cols, W), bf16),
            jax.ShapeDtypeStruct((side // 8, side), bf16),
        ),
        in_specs=[smem, smem, smem, hbm, hbm, hbm, vmem, vmem],
        out_specs=(vmem, vmem),
        scratch_shapes=[
            pltpu.VMEM((W, W), f32),
            pltpu.VMEM((W, cols), f32),
            pltpu.VMEM((NB - 1, W, W), bf16),
            pltpu.VMEM((NB - 1, QUAD, W, W), bf16),
            pltpu.VMEM((QUAD, share, W), f32),
            pltpu.VMEM((QUAD, share, W), bf16),
            pltpu.VMEM((cols, W), bf16),
            pltpu.VMEM((NB, NODES, share, W), bf16),
            pltpu.VMEM((NB, share, W), bf16),
            pltpu.VMEM((W, W), bf16),
            pltpu.VMEM((W, W), bf16),
            pltpu.VMEM((QUAD, share, W), bf16),
            pltpu.VMEM((cols, W), bf16),
            pltpu.VMEM((share, side), bf16),
            pltpu.VMEM((side, side // NODES), bf16),
            pltpu.VMEM((ranks - 1, side // ranks, side // NODES), bf16),
            pltpu.VMEM((side // ranks, side // NODES), bf16),
            pltpu.VMEM((side // 8, side), bf16),
            dma((2,)),
            dma((NB - 1,)),
            dma((3,)), dma((3,)),
            dma((NB - 1, 3)), dma((NB - 1, 3)),
            dma((NB - 1,)), dma((NB - 1,)),
            dma((NB - 1, 2)), dma((NB - 1, 2)),
            dma((NB, HALVES, 3)), dma((NB, HALVES, 3)),
            dma((3,)), dma((3,)),
            dma((ranks - 1,)), dma((ranks - 1,)),
            dma((NB - 1,)), dma((NB - 1,)),
        ],
        compiler_params=pltpu.CompilerParams(
            collective_id=0, has_side_effects=True, vmem_limit_bytes=60 * 1024 * 1024
        ),
        name="substitute",
    )(block_order, panel_pair, lengthscale, factor_rows, diag_inverse, carried, inducing, data_points)
    return finish(solved_t, gram)


def solution(mesh):
    in_specs = (
        P("ind", None),
        P("ind", None),
        P(None, "ind"),
        P(None, "dp"),
        P(),
        P("ind", "dp"),
        P(),
        P(),
    )
    out_specs = (P("ind", "dp"), P("dp", None))
    return jax.shard_map(
        on_device, mesh=mesh, in_specs=in_specs, out_specs=out_specs, check_vma=False
    )
```

```python
import functools

import jax
import jax.numpy as jnp
from jax import lax
from jax.experimental import pallas as pl
from jax.experimental.pallas import tpu as pltpu
from jax.sharding import PartitionSpec as P

MESH = pl.DeviceIdType.MESH
TT = (((0,), (1,)), ((), ()))
TN = (((0,), (0,)), ((), ()))
f32 = jnp.float32
bf16 = jnp.bfloat16

NB, W, NODES, QUAD = 16, 512, 4, 4
SOON, LEAD, HALVES, FIRST = 3, 6, 4, 0


def kernel(
    order, pair, scales, factor, inverse_hbm, carried_hbm, inducing, points, solved_t, gram,
    dinv, carried, stage, fact, ycur, yin, y0t, cand, xall, fcrit, dbf, xq, solt, st, parts, inbox, piece, tile,
    i_sem, n_sem, y_s, y_r, f_s, f_r, l_s, l_r, z_s, z_r, c_s, c_r, s_s, s_r, g_s, g_r, o_s, o_r,
):
    cols = points.shape[1]
    share = cols // QUAD
    dp = lax.axis_index("dp")
    me = lax.axis_index("ind")
    node = lax.div(me, QUAD)
    q = lax.rem(me, QUAD)
    core = lax.rem(q, 2)
    xlo = lax.div(q, 2)
    q1 = 2 * xlo + 1 - core
    q2 = 2 * (1 - xlo) + core
    q3 = 2 * (1 - xlo) + 1 - core
    base = node * QUAD
    up = lax.rem(node + 1, NODES) * QUAD + q
    down = lax.rem(node + NODES - 1, NODES) * QUAD + q
    across = lax.rem(node + 2, NODES) * QUAD + q
    other_dp = dp + 1 - 2 * lax.rem(dp, 2)
    z_next = lax.rem(dp + 2, 8)
    z_last = lax.rem(dp + 6, 8)
    parity = lax.rem(lax.div(dp, 2), 2)
    rank = dp * QUAD + q
    ranks = 8 * QUAD

    def at(d, i):
        return {"dp": d, "ind": i}

    def remote(src, dst, ssem, rsem, dev):
        return pltpu.make_async_remote_copy(
            src_ref=src, dst_ref=dst, send_sem=ssem, recv_sem=rsem,
            device_id=dev, device_id_type=MESH,
        )

    def n_copy(b):
        return pltpu.make_async_copy(
            factor.at[:, pl.ds(pl.multiple_of(b * W, W), W)], stage.at[b], n_sem.at[b]
        )

    d_copy = pltpu.make_async_copy(inverse_hbm, dinv, i_sem.at[0])
    r_copy = pltpu.make_async_copy(carried_hbm, carried, i_sem.at[1])
    d_copy.start()
    n_copy(0).start()
    r_copy.start()

    @pl.loop(1, NB - 1)
    def _(b):
        n_copy(b).start()

    barrier = pltpu.get_barrier_semaphore()
    near = (
        at(dp, up), at(dp, down), at(dp, across), at(dp, base + q2), at(other_dp, base + q2),
        at(z_next, me), at(z_last, me), at(dp, base + q3), at(dp, base + q1),
    )
    for device in near:
        pl.semaphore_signal(barrier, inc=1, device_id=device, device_id_type=MESH)

    def compute(b):
        n_copy(b).wait()
        fact[b, q] = lax.dot_general(stage[b], dbf[...], TT, preferred_element_type=f32).astype(bf16)

    d_copy.wait()
    dbf[...] = dinv[...].astype(bf16)
    compute(0)

    along = inducing[...].T
    distance = jnp.zeros((W, cols), f32)
    for feature in range(points.shape[0]):
        inverse = jnp.full((1, 1), 1.0, f32) / scales[feature]
        offset = (along[:, feature : feature + 1] - points[feature : feature + 1, :]) * inverse
        distance = distance + offset * offset
    r_copy.wait()
    residual = jnp.exp(-0.5 * distance) - carried[...]
    y0 = jnp.dot(dinv[...], residual, precision=lax.Precision.HIGHEST, preferred_element_type=f32)
    y0 = y0.T
    y0t[...] = y0.astype(bf16)

    pl.semaphore_wait(barrier, len(near))

    quad = (q2, q3, q1)

    half = share // HALVES

    def y_copy(k, h):
        to = quad[k]
        return remote(
            y0t.at[pl.ds(pl.multiple_of(to * share + h * half, half), half)], yin.at[q, pl.ds(h * half, half)],
            y_s.at[h, k], y_r.at[h, k], at(dp, base + to),
        )


    part = W // 4
    q_a = pl.ds(pl.multiple_of(2 * parity * part, part), part)
    q_b = pl.ds(pl.multiple_of((2 * parity + 1) * part, part), part)

    def f_copies(b):
        return (
            remote(fact.at[b, q, q_a], fact.at[b, q, q_a], f_s.at[b, 0], f_r.at[b, 0], at(dp, base + q2)),
            remote(fact.at[b, q, q_b], fact.at[b, q, q_b], f_s.at[b, 1], f_r.at[b, 1], at(other_dp, base + q2)),
            remote(fact.at[b, q], fact.at[b, q], f_s.at[b, 2], f_r.at[b, 2], at(dp, base + q1)),
        )

    def z_copies(b):
        return (
            remote(fact.at[b, q2, q_a], fact.at[b, q2, q_a], z_s.at[b, 0], z_r.at[b, 0], at(z_last, me)),
            remote(fact.at[b, q2, q_b], fact.at[b, q2, q_b], z_s.at[b, 1], z_r.at[b, 1], at(z_next, me)),
        )

    mine_x = pl.ds(pl.multiple_of(2 * parity * part, part), 2 * part)
    mine_z = pl.ds(pl.multiple_of(2 * (1 - parity) * part, part), 2 * part)

    def relays(b):
        return tuple(
            remote(fact.at[b, q2, rows], fact.at[b, q2, rows], l_s.at[b, n], l_r.at[b, n], at(dp, base + q1))
            for n, rows in enumerate((mine_x, mine_z))
        )

    def share_z(b):
        for got, on in zip(f_copies(b), z_copies(b)):
            got.wait_recv()
            on.start()
        relays(b)[0].start()

    def share_core(b):
        for got in z_copies(b):
            got.wait_recv()
        relays(b)[1].start()

    def send(b):
        for copy in f_copies(b):
            copy.start()

    def make(b):
        compute(b)
        send(b)


    def c_copies(b, h):
        rows = pl.ds(h * half, half)
        return tuple(
            remote(cand.at[b, 0, rows], cand.at[b, n + 1, rows], c_s.at[b, h, n], c_r.at[b, h, n], at(dp, to))
            for n, to in ((2, across), (0, up), (1, down))
        )

    def offer(b, h, value):
        cand[b, 0, pl.ds(h * half, half)] = value.astype(bf16)
        for copy in c_copies(b, h):
            copy.start()

    def choose(b, h):
        rows = pl.ds(h * half, half)
        for got in c_copies(b, h):
            got.wait_recv()
        away = lax.rem(lax.div(order[b], QUAD) - node + NODES, NODES)
        x = jnp.where(
            away == 0, cand[b, 0, rows],
            jnp.where(away == 3, cand[b, 1, rows], jnp.where(away == 1, cand[b, 2, rows], cand[b, 3, rows])),
        )
        xall[b, rows] = x
        return x

    for h in range(HALVES):
        if h == FIRST:
            send(0)
        for k in range(3):
            y_copy(k, h).start()
    ycur[q] = y0t[pl.ds(pl.multiple_of(q * share, share), share), :].astype(f32)

    def f_sent(b):
        for copy in f_copies(b) + z_copies(b) + relays(b):
            copy.wait_send()

    def c_sent(b):
        for h in range(HALVES):
            for copy in c_copies(b, h):
                copy.wait_send()

    @pl.loop(1, SOON)
    def _(b):
        make(b)

    share_z(0)
    first = lax.rem(order[0], QUAD)
    for h in range(HALVES):
        rows = pl.ds(h * half, half)
        for k in range(3):
            y_copy(k, h).wait_recv()
            ycur[quad[k], rows] = yin[quad[k], rows].astype(f32)
        offer(0, h, ycur[first, rows])

    @pl.loop(SOON, LEAD)
    def _(b):
        make(b)

    share_core(0)
    share_z(1)
    early = {
        1: ((share_z, 2), (share_core, 1)),
        2: ((share_z, 3), (share_core, 2), (share_z, 4)),
        3: ((share_core, 3), (share_z, 5), (share_core, 4), (share_z, 6)),
    }

    @pl.loop(0, NB - 1)
    def _(b):
        for step, work in early.items():
            @pl.when(b == step)
            def _():
                for share, block in work:
                    share(block)

        @pl.when((b > max(early)) & (b + 3 < NB - 1))
        def _():
            share_z(b + 3)

        @pl.when((b > max(early)) & (b + 1 < NB - 1))
        def _():
            share_core(b + 1)

        f_copies(b)[2].wait_recv()
        for got in relays(b):
            got.wait_recv()
        following = lax.rem(order[b + 1], QUAD)
        fcrit[...] = jnp.where(
            following == 0, fact[b, 0],
            jnp.where(following == 1, fact[b, 1], jnp.where(following == 2, fact[b, 2], fact[b, 3])),
        )
        for h in range(HALVES):
            x = choose(b, h)
            known = ycur[following, pl.ds(h * half, half)]
            offer(b + 1, h, known - jnp.dot(x, fcrit[...], preferred_element_type=f32))
        for j in range(QUAD):
            ycur[j] = ycur[j] - jnp.dot(xall[b], fact[b, j], preferred_element_type=f32)

        @pl.when(b + LEAD < NB - 1)
        def _():
            make(b + LEAD)

        c_sent(b)

        @pl.when(b > 0)
        def _():
            f_sent(b - 1)

    for h in range(HALVES):
        choose(NB - 1, h)

    st[:, :W] = xall[pair[0]]
    st[:, W:] = xall[pair[1]]
    wide = gram.shape[1] // NODES
    tall = parts.shape[0] // ranks
    my_cols = pl.ds(pl.multiple_of(node * wide, wide), wide)
    parts[...] = lax.dot_general(st[...], st[:, my_cols], TN, preferred_element_type=f32).astype(bf16)

    def g_copy(k):
        t = lax.rem(rank + k, ranks)
        return remote(
            parts.at[pl.ds(pl.multiple_of(t * tall, tall), tall)], inbox.at[k - 1],
            g_s.at[k - 1], g_r.at[k - 1], at(lax.div(t, QUAD), base + lax.rem(t, QUAD)),
        )

    @pl.loop(1, ranks)
    def _(k):
        g_copy(k).start()

    for j in range(QUAD):
        place = jnp.int32(0)
        for b in range(NB):
            place = jnp.where(order[b] == base + j, b, place)
        xq[j] = xall[place]
    mine = pl.ds(pl.multiple_of(q * share, share), share)

    def s_copy(k):
        return remote(xq.at[quad[k]], solt.at[mine], s_s.at[k], s_r.at[k], at(dp, base + quad[k]))

    for k in range(3):
        s_copy(k).start()
    solt[mine, :] = xq[q]

    total = parts[pl.ds(pl.multiple_of(rank * tall, tall), tall), :].astype(f32)

    def add(k, total):
        g_copy(k).wait_recv()
        return total + inbox[k - 1].astype(f32)

    total = lax.fori_loop(1, ranks, add, total)
    row = rank * tall + lax.broadcasted_iota(jnp.int32, (tall, wide), 0)
    col = node * wide + lax.broadcasted_iota(jnp.int32, (tall, wide), 1)
    scale = 1.0 / (cols * 8)
    result = jnp.where(row >= col, total * scale, 0.0).astype(bf16)
    piece[...] = result
    my_rows = pl.ds(pl.multiple_of(q * tall, tall), tall)

    def o_copy(k):
        return remote(
            piece, tile.at[my_rows, my_cols], o_s.at[k - 1], o_r.at[k - 1], at(dp, lax.rem(me + k, NB))
        )

    @pl.loop(1, NB)
    def _(k):
        o_copy(k).start()

    tile[my_rows, my_cols] = result

    for k in range(3):
        s_copy(k).wait_recv()
    solved_t[...] = solt[...]

    f_sent(NB - 2)
    c_sent(NB - 1)

    for k in range(3):
        for h in range(HALVES):
            y_copy(k, h).wait_send()
        s_copy(k).wait_send()

    @pl.loop(1, ranks)
    def _(k):
        g_copy(k).wait_send()

    @pl.loop(1, NB)
    def _(k):
        o_copy(k).wait()

    gram[...] = tile[...]


def finish(solved_t, gram):
    def body(solved_t, gram, solved, gram_out):
        solved[...] = solved_t[...].T
        gram_out[...] = gram[...].astype(f32)

    cols, rows = solved_t.shape
    return pl.pallas_call(
        body,
        out_shape=(jax.ShapeDtypeStruct((rows, cols), bf16), jax.ShapeDtypeStruct(gram.shape, f32)),
        name="finish",
    )(solved_t, gram)


def on_device(factor_rows, diag_inverse, inducing, data_points, lengthscale, carried, block_order, panel_pair):
    cols = data_points.shape[1]
    share = cols // QUAD
    ranks = 8 * QUAD
    side = 2 * W
    smem = pl.BlockSpec(memory_space=pltpu.SMEM)
    vmem = pl.BlockSpec(memory_space=pltpu.VMEM)
    hbm = pl.BlockSpec(memory_space=pl.ANY)
    dma = pltpu.SemaphoreType.DMA
    solved_t, gram = pl.pallas_call(
        kernel,
        out_shape=(
            jax.ShapeDtypeStruct((cols, W), bf16),
            jax.ShapeDtypeStruct((side // 8, side), bf16),
        ),
        in_specs=[smem, smem, smem, hbm, hbm, hbm, vmem, vmem],
        out_specs=(vmem, vmem),
        scratch_shapes=[
            pltpu.VMEM((W, W), f32),
            pltpu.VMEM((W, cols), f32),
            pltpu.VMEM((NB - 1, W, W), bf16),
            pltpu.VMEM((NB - 1, QUAD, W, W), bf16),
            pltpu.VMEM((QUAD, share, W), f32),
            pltpu.VMEM((QUAD, share, W), bf16),
            pltpu.VMEM((cols, W), bf16),
            pltpu.VMEM((NB, NODES, share, W), bf16),
            pltpu.VMEM((NB, share, W), bf16),
            pltpu.VMEM((W, W), bf16),
            pltpu.VMEM((W, W), bf16),
            pltpu.VMEM((QUAD, share, W), bf16),
            pltpu.VMEM((cols, W), bf16),
            pltpu.VMEM((share, side), bf16),
            pltpu.VMEM((side, side // NODES), bf16),
            pltpu.VMEM((ranks - 1, side // ranks, side // NODES), bf16),
            pltpu.VMEM((side // ranks, side // NODES), bf16),
            pltpu.VMEM((side // 8, side), bf16),
            dma((2,)),
            dma((NB - 1,)),
            dma((HALVES, 3)), dma((HALVES, 3)),
            dma((NB - 1, 3)), dma((NB - 1, 3)),
            dma((NB - 1, 2)), dma((NB - 1, 2)),
            dma((NB - 1, 2)), dma((NB - 1, 2)),
            dma((NB, HALVES, 3)), dma((NB, HALVES, 3)),
            dma((3,)), dma((3,)),
            dma((ranks - 1,)), dma((ranks - 1,)),
            dma((NB - 1,)), dma((NB - 1,)),
        ],
        compiler_params=pltpu.CompilerParams(
            collective_id=0, has_side_effects=True, vmem_limit_bytes=60 * 1024 * 1024
        ),
        name="substitute",
    )(block_order, panel_pair, lengthscale, factor_rows, diag_inverse, carried, inducing, data_points)
    return finish(solved_t, gram)


def solution(mesh):
    in_specs = (
        P("ind", None),
        P("ind", None),
        P(None, "ind"),
        P(None, "dp"),
        P(),
        P("ind", "dp"),
        P(),
        P(),
    )
    out_specs = (P("ind", "dp"), P("dp", None))
    return jax.shard_map(
        on_device, mesh=mesh, in_specs=in_specs, out_specs=out_specs, check_vma=False
    )
```

```python
import functools

import jax
import jax.numpy as jnp
from jax import lax
from jax.experimental import pallas as pl
from jax.experimental.pallas import tpu as pltpu
from jax.sharding import PartitionSpec as P

MESH = pl.DeviceIdType.MESH
TT = (((0,), (1,)), ((), ()))
TN = (((0,), (0,)), ((), ()))
f32 = jnp.float32
bf16 = jnp.bfloat16

NB, W, NODES, QUAD = 16, 512, 4, 4
SOON, LEAD, HALVES, FIRST = 4, 7, 4, 0


def kernel(
    order, pair, scales, factor, inverse_hbm, carried_hbm, inducing, points, solved_t, gram,
    dinv, carried, stage, fact, ycur, yin, y0t, cand, xall, fcrit, dbf, xq, solt, st, parts, inbox, piece, tile,
    i_sem, n_sem, y_s, y_r, f_s, f_r, l_s, l_r, z_s, z_r, c_s, c_r, s_s, s_r, g_s, g_r, o_s, o_r,
):
    cols = points.shape[1]
    share = cols // QUAD
    dp = lax.axis_index("dp")
    me = lax.axis_index("ind")
    node = lax.div(me, QUAD)
    q = lax.rem(me, QUAD)
    core = lax.rem(q, 2)
    xlo = lax.div(q, 2)
    q1 = 2 * xlo + 1 - core
    q2 = 2 * (1 - xlo) + core
    q3 = 2 * (1 - xlo) + 1 - core
    base = node * QUAD
    up = lax.rem(node + 1, NODES) * QUAD + q
    down = lax.rem(node + NODES - 1, NODES) * QUAD + q
    across = lax.rem(node + 2, NODES) * QUAD + q
    other_dp = dp + 1 - 2 * lax.rem(dp, 2)
    z_next = lax.rem(dp + 2, 8)
    z_last = lax.rem(dp + 6, 8)
    parity = lax.rem(lax.div(dp, 2), 2)
    rank = dp * QUAD + q
    ranks = 8 * QUAD

    def at(d, i):
        return {"dp": d, "ind": i}

    def remote(src, dst, ssem, rsem, dev):
        return pltpu.make_async_remote_copy(
            src_ref=src, dst_ref=dst, send_sem=ssem, recv_sem=rsem,
            device_id=dev, device_id_type=MESH,
        )

    def n_copy(b):
        return pltpu.make_async_copy(
            factor.at[:, pl.ds(pl.multiple_of(b * W, W), W)], stage.at[b], n_sem.at[b]
        )

    d_copy = pltpu.make_async_copy(inverse_hbm, dinv, i_sem.at[0])
    r_copy = pltpu.make_async_copy(carried_hbm, carried, i_sem.at[1])
    d_copy.start()
    n_copy(0).start()
    r_copy.start()

    @pl.loop(1, NB - 1)
    def _(b):
        n_copy(b).start()

    barrier = pltpu.get_barrier_semaphore()
    near = (
        at(dp, up), at(dp, down), at(dp, across), at(dp, base + q2), at(other_dp, base + q2),
        at(z_next, me), at(z_last, me), at(dp, base + q3), at(dp, base + q1),
    )
    for device in near:
        pl.semaphore_signal(barrier, inc=1, device_id=device, device_id_type=MESH)

    def compute(b):
        n_copy(b).wait()
        fact[b, q] = lax.dot_general(stage[b], dbf[...], TT, preferred_element_type=f32).astype(bf16)

    d_copy.wait()
    dbf[...] = dinv[...].astype(bf16)
    compute(0)

    along = inducing[...].T
    distance = jnp.zeros((W, cols), f32)
    for feature in range(points.shape[0]):
        inverse = jnp.full((1, 1), 1.0, f32) / scales[feature]
        offset = (along[:, feature : feature + 1] - points[feature : feature + 1, :]) * inverse
        distance = distance + offset * offset
    r_copy.wait()
    residual = jnp.exp(-0.5 * distance) - carried[...]
    y0 = jnp.dot(dinv[...], residual, precision=lax.Precision.HIGHEST, preferred_element_type=f32)
    y0 = y0.T
    y0t[...] = y0.astype(bf16)

    pl.semaphore_wait(barrier, len(near))

    quad = (q2, q3, q1)

    half = share // HALVES

    def y_copy(k, h):
        to = quad[k]
        return remote(
            y0t.at[pl.ds(pl.multiple_of(to * share + h * half, half), half)], yin.at[q, pl.ds(h * half, half)],
            y_s.at[h, k], y_r.at[h, k], at(dp, base + to),
        )


    part = W // 4
    q_a = pl.ds(pl.multiple_of(2 * parity * part, part), part)
    q_b = pl.ds(pl.multiple_of((2 * parity + 1) * part, part), part)

    def f_copies(b):
        return (
            remote(fact.at[b, q, q_a], fact.at[b, q, q_a], f_s.at[b, 0], f_r.at[b, 0], at(dp, base + q2)),
            remote(fact.at[b, q, q_b], fact.at[b, q, q_b], f_s.at[b, 1], f_r.at[b, 1], at(other_dp, base + q2)),
            remote(fact.at[b, q], fact.at[b, q], f_s.at[b, 2], f_r.at[b, 2], at(dp, base + q1)),
        )

    def z_copies(b):
        return (
            remote(fact.at[b, q2, q_a], fact.at[b, q2, q_a], z_s.at[b, 0], z_r.at[b, 0], at(z_last, me)),
            remote(fact.at[b, q2, q_b], fact.at[b, q2, q_b], z_s.at[b, 1], z_r.at[b, 1], at(z_next, me)),
        )

    mine_x = pl.ds(pl.multiple_of(2 * parity * part, part), 2 * part)
    mine_z = pl.ds(pl.multiple_of(2 * (1 - parity) * part, part), 2 * part)

    def relays(b):
        return tuple(
            remote(fact.at[b, q2, rows], fact.at[b, q2, rows], l_s.at[b, n], l_r.at[b, n], at(dp, base + q1))
            for n, rows in enumerate((mine_x, mine_z))
        )

    def share_z(b):
        for got, on in zip(f_copies(b), z_copies(b)):
            got.wait_recv()
            on.start()
        relays(b)[0].start()

    def share_core(b):
        for got in z_copies(b):
            got.wait_recv()
        relays(b)[1].start()

    def send(b):
        for copy in f_copies(b):
            copy.start()

    def make(b):
        compute(b)
        send(b)


    def c_copies(b, h):
        rows = pl.ds(h * half, half)
        return tuple(
            remote(cand.at[b, 0, rows], cand.at[b, n + 1, rows], c_s.at[b, h, n], c_r.at[b, h, n], at(dp, to))
            for n, to in ((2, across), (0, up), (1, down))
        )

    def offer(b, h, value):
        cand[b, 0, pl.ds(h * half, half)] = value.astype(bf16)
        for copy in c_copies(b, h):
            copy.start()

    def choose(b, h):
        rows = pl.ds(h * half, half)
        for got in c_copies(b, h):
            got.wait_recv()
        away = lax.rem(lax.div(order[b], QUAD) - node + NODES, NODES)
        x = jnp.where(
            away == 0, cand[b, 0, rows],
            jnp.where(away == 3, cand[b, 1, rows], jnp.where(away == 1, cand[b, 2, rows], cand[b, 3, rows])),
        )
        xall[b, rows] = x
        return x

    for h in range(HALVES):
        if h == FIRST:
            send(0)
        for k in range(3):
            y_copy(k, h).start()
    ycur[q] = y0t[pl.ds(pl.multiple_of(q * share, share), share), :].astype(f32)

    def f_sent(b):
        for copy in f_copies(b) + z_copies(b) + relays(b):
            copy.wait_send()

    def c_sent(b):
        for h in range(HALVES):
            for copy in c_copies(b, h):
                copy.wait_send()

    @pl.loop(1, SOON)
    def _(b):
        make(b)

    share_z(0)
    first = lax.rem(order[0], QUAD)
    for h in range(HALVES):
        rows = pl.ds(h * half, half)
        for k in range(3):
            y_copy(k, h).wait_recv()
            ycur[quad[k], rows] = yin[quad[k], rows].astype(f32)
        offer(0, h, ycur[first, rows])

    @pl.loop(SOON, LEAD)
    def _(b):
        make(b)

    share_core(0)
    share_z(1)
    early = {
        1: ((share_z, 2), (share_core, 1)),
        2: ((share_z, 3), (share_core, 2), (share_z, 4)),
        3: ((share_core, 3), (share_z, 5), (share_core, 4), (share_z, 6)),
    }

    @pl.loop(0, NB - 1)
    def _(b):
        for step, work in early.items():
            @pl.when(b == step)
            def _():
                for share, block in work:
                    share(block)

        @pl.when((b > max(early)) & (b + 3 < NB - 1))
        def _():
            share_z(b + 3)

        @pl.when((b > max(early)) & (b + 1 < NB - 1))
        def _():
            share_core(b + 1)

        f_copies(b)[2].wait_recv()
        for got in relays(b):
            got.wait_recv()
        following = lax.rem(order[b + 1], QUAD)
        fcrit[...] = jnp.where(
            following == 0, fact[b, 0],
            jnp.where(following == 1, fact[b, 1], jnp.where(following == 2, fact[b, 2], fact[b, 3])),
        )
        for h in range(HALVES):
            x = choose(b, h)
            known = ycur[following, pl.ds(h * half, half)]
            offer(b + 1, h, known - jnp.dot(x, fcrit[...], preferred_element_type=f32))
        for j in range(QUAD):
            ycur[j] = ycur[j] - jnp.dot(xall[b], fact[b, j], preferred_element_type=f32)

        @pl.when(b + LEAD < NB - 1)
        def _():
            make(b + LEAD)

        c_sent(b)

        @pl.when(b > 0)
        def _():
            f_sent(b - 1)

    for h in range(HALVES):
        choose(NB - 1, h)

    st[:, :W] = xall[pair[0]]
    st[:, W:] = xall[pair[1]]
    wide = gram.shape[1] // NODES
    tall = parts.shape[0] // ranks
    my_cols = pl.ds(pl.multiple_of(node * wide, wide), wide)
    parts[...] = lax.dot_general(st[...], st[:, my_cols], TN, preferred_element_type=f32).astype(bf16)

    def g_copy(k):
        t = lax.rem(rank + k, ranks)
        return remote(
            parts.at[pl.ds(pl.multiple_of(t * tall, tall), tall)], inbox.at[k - 1],
            g_s.at[k - 1], g_r.at[k - 1], at(lax.div(t, QUAD), base + lax.rem(t, QUAD)),
        )

    @pl.loop(1, ranks)
    def _(k):
        g_copy(k).start()

    for j in range(QUAD):
        place = jnp.int32(0)
        for b in range(NB):
            place = jnp.where(order[b] == base + j, b, place)
        xq[j] = xall[place]
    mine = pl.ds(pl.multiple_of(q * share, share), share)

    def s_copy(k):
        return remote(xq.at[quad[k]], solt.at[mine], s_s.at[k], s_r.at[k], at(dp, base + quad[k]))

    for k in range(3):
        s_copy(k).start()
    solt[mine, :] = xq[q]

    total = parts[pl.ds(pl.multiple_of(rank * tall, tall), tall), :].astype(f32)

    def add(k, total):
        g_copy(k).wait_recv()
        return total + inbox[k - 1].astype(f32)

    total = lax.fori_loop(1, ranks, add, total)
    row = rank * tall + lax.broadcasted_iota(jnp.int32, (tall, wide), 0)
    col = node * wide + lax.broadcasted_iota(jnp.int32, (tall, wide), 1)
    scale = 1.0 / (cols * 8)
    result = jnp.where(row >= col, total * scale, 0.0).astype(bf16)
    piece[...] = result
    my_rows = pl.ds(pl.multiple_of(q * tall, tall), tall)

    def o_copy(k):
        return remote(
            piece, tile.at[my_rows, my_cols], o_s.at[k - 1], o_r.at[k - 1], at(dp, lax.rem(me + k, NB))
        )

    @pl.loop(1, NB)
    def _(k):
        o_copy(k).start()

    tile[my_rows, my_cols] = result

    for k in range(3):
        s_copy(k).wait_recv()
    solved_t[...] = solt[...]

    f_sent(NB - 2)
    c_sent(NB - 1)

    for k in range(3):
        for h in range(HALVES):
            y_copy(k, h).wait_send()
        s_copy(k).wait_send()

    @pl.loop(1, ranks)
    def _(k):
        g_copy(k).wait_send()

    @pl.loop(1, NB)
    def _(k):
        o_copy(k).wait()

    gram[...] = tile[...]


def finish(solved_t, gram):
    def body(solved_t, gram, solved, gram_out):
        solved[...] = solved_t[...].T
        gram_out[...] = gram[...].astype(f32)

    cols, rows = solved_t.shape
    return pl.pallas_call(
        body,
        out_shape=(jax.ShapeDtypeStruct((rows, cols), bf16), jax.ShapeDtypeStruct(gram.shape, f32)),
        name="finish",
    )(solved_t, gram)


def on_device(factor_rows, diag_inverse, inducing, data_points, lengthscale, carried, block_order, panel_pair):
    cols = data_points.shape[1]
    share = cols // QUAD
    ranks = 8 * QUAD
    side = 2 * W
    smem = pl.BlockSpec(memory_space=pltpu.SMEM)
    vmem = pl.BlockSpec(memory_space=pltpu.VMEM)
    hbm = pl.BlockSpec(memory_space=pl.ANY)
    dma = pltpu.SemaphoreType.DMA
    solved_t, gram = pl.pallas_call(
        kernel,
        out_shape=(
            jax.ShapeDtypeStruct((cols, W), bf16),
            jax.ShapeDtypeStruct((side // 8, side), bf16),
        ),
        in_specs=[smem, smem, smem, hbm, hbm, hbm, vmem, vmem],
        out_specs=(vmem, vmem),
        scratch_shapes=[
            pltpu.VMEM((W, W), f32),
            pltpu.VMEM((W, cols), f32),
            pltpu.VMEM((NB - 1, W, W), bf16),
            pltpu.VMEM((NB - 1, QUAD, W, W), bf16),
            pltpu.VMEM((QUAD, share, W), f32),
            pltpu.VMEM((QUAD, share, W), bf16),
            pltpu.VMEM((cols, W), bf16),
            pltpu.VMEM((NB, NODES, share, W), bf16),
            pltpu.VMEM((NB, share, W), bf16),
            pltpu.VMEM((W, W), bf16),
            pltpu.VMEM((W, W), bf16),
            pltpu.VMEM((QUAD, share, W), bf16),
            pltpu.VMEM((cols, W), bf16),
            pltpu.VMEM((share, side), bf16),
            pltpu.VMEM((side, side // NODES), bf16),
            pltpu.VMEM((ranks - 1, side // ranks, side // NODES), bf16),
            pltpu.VMEM((side // ranks, side // NODES), bf16),
            pltpu.VMEM((side // 8, side), bf16),
            dma((2,)),
            dma((NB - 1,)),
            dma((HALVES, 3)), dma((HALVES, 3)),
            dma((NB - 1, 3)), dma((NB - 1, 3)),
            dma((NB - 1, 2)), dma((NB - 1, 2)),
            dma((NB - 1, 2)), dma((NB - 1, 2)),
            dma((NB, HALVES, 3)), dma((NB, HALVES, 3)),
            dma((3,)), dma((3,)),
            dma((ranks - 1,)), dma((ranks - 1,)),
            dma((NB - 1,)), dma((NB - 1,)),
        ],
        compiler_params=pltpu.CompilerParams(
            collective_id=0, has_side_effects=True, vmem_limit_bytes=60 * 1024 * 1024
        ),
        name="substitute",
    )(block_order, panel_pair, lengthscale, factor_rows, diag_inverse, carried, inducing, data_points)
    return finish(solved_t, gram)


def solution(mesh):
    in_specs = (
        P("ind", None),
        P("ind", None),
        P(None, "ind"),
        P(None, "dp"),
        P(),
        P("ind", "dp"),
        P(),
        P(),
    )
    out_specs = (P("ind", "dp"), P("dp", None))
    return jax.shard_map(
        on_device, mesh=mesh, in_specs=in_specs, out_specs=out_specs, check_vma=False
    )
```
